32 devices in a mesh: groups: 2 (over y), ctx: 4 (over z), exp: 2 (over x), tp: 2 (over core).
Axes of the slice: x: 2, y: 2, z: 4, core: 2. Of those that a mesh axis runs over, the one named last changes fastest.
Arguments:
- queries: bfloat16 [4, 512, 20, 128], P(('groups', 'exp'), 'ctx', 'tp'), parts along dimension 0, may hold values from -9 to 9
- key_states: bfloat16 [4, 512, 4, 128], P(('groups', 'exp'), 'ctx', 'tp'), parts along dimension 0, may hold values from -9 to 9
- values: bfloat16 [4, 512, 4, 128], P(('groups', 'exp'), 'ctx', 'tp'), parts along dimension 0, may hold values from -6 to 6
- doc_ids: int32 [4, 512], P(('groups', 'exp'), 'ctx'), parts along dimension 0, may hold values from 0 to 3, never falling along the last dimension, each value on 1 to 256 neighbouring positions
- residual: bfloat16 [4, 512, 5120], P(('groups', 'exp'), ('ctx', 'tp')), parts along dimension 0, may hold values from -6 to 6
- out_proj: bfloat16 [2560, 5120], P('tp', 'ctx'), may hold values from -0.125 to 0.125
- norm_gain: bfloat16 [5120], replicated, may hold values from 0.5 to 1.5
- router: bfloat16 [5120, 64], P(None, 'exp'), may hold values from -0.078125 to 0.078125
- expert_ids: int32 [4, 512, 1], P(('groups', 'exp'), ('ctx', 'tp')), parts along dimension 0, may hold values from 0 to 63; in each aligned block of 64 rows (0 to 63, 64 to 127, ..., all dimensions but the last counted through in order) at most 2 rows name the same one
- keep_counts: int32 [128], P('groups'), parts along dimension 0, may hold values from 1 to 2
Outputs:
- expert_inputs: bfloat16 [32, 64, 2, 5120], P(('groups', 'ctx', 'tp'), 'exp'), parts along dimension 0
The draws below stay inside these ranges and needn't reach their ends.
There are 2 independent parts, one for each index of `groups`. The reference program is written for one: setup_inputs(seed, part) draws one part's arguments, and reference() takes and returns one part's arrays. A program takes and returns all parts, laid end to end along the dimension named above; an argument that names none is the same for every part. Nothing has to cross between parts.
Inputs may be any that keep to these rules, and one draw needn't show every extreme that they name: `doc_ids`: doc ids never fall along a request; a document holds at most 256 tokens, and some document holds exactly that many. `expert_ids`: in each aligned block of 64 tokens (the rows of one device) no expert is named more than 2 times, and in some blocks one expert is named exactly 2 times.
All inputs are finite; a program needn't handle non-finite values.
Results may differ from the reference program's by a relative error of at most 0.013.
Values may be sent and summed in bfloat16 or wider, within the bound.
A program may use at most 64 MiB of HBM per device.

```python
import math
import jax
import jax.numpy as jnp
import numpy as np
from jax import lax

D = 5120
HEAD_DIMENSION = 128
EXPERTS = 64
QUERY_HEADS = 20
KEY_VALUE_HEADS = 4
CAP = 2
DOCS = 4
TOK_DEV = 128
REQUEST_COUNT = 2
REQUEST_TOKENS = 512
N_CTX = 4
N_TP = 2


def query_key_pair(key):
    folded = jax.random.fold_in(key, 5)
    query_key, state_random_key = jax.random.split(folded, 2)
    sampled_query = jnp.clip(jax.random.normal(query_key, (REQUEST_COUNT, REQUEST_TOKENS, QUERY_HEADS, HEAD_DIMENSION), jnp.float32), -4.0, 4.0)
    sampled_state = jnp.clip(jax.random.normal(state_random_key, (REQUEST_COUNT, REQUEST_TOKENS, KEY_VALUE_HEADS, HEAD_DIMENSION), jnp.float32), -4.0, 4.0)
    return (sampled_query, sampled_state)


def draw_queries(key, part):
    return query_key_pair(key)[0].astype(jnp.bfloat16)


def draw_key_states(key, part):
    return query_key_pair(key)[1].astype(jnp.bfloat16)


def draw_residual(key, part):
    folded = jax.random.fold_in(key, 11)
    noise_key, row_key, column_key = jax.random.split(folded, 3)
    row_scale = jnp.exp(jax.random.uniform(row_key, (REQUEST_COUNT, REQUEST_TOKENS, 1), jnp.float32, math.log(0.02), math.log(0.2)))
    column_scale = jnp.exp(jax.random.uniform(column_key, (1, 1, D), jnp.float32, math.log(0.33), math.log(3.3)))
    noise = jnp.clip(jax.random.normal(noise_key, (REQUEST_COUNT, REQUEST_TOKENS, D), jnp.float32), -4.0, 4.0)
    return (noise * row_scale * column_scale).astype(jnp.bfloat16)


def plant(result, own_key, least, largest):
    longest = result.shape.index(max(result.shape))
    spots = []
    for shift in (0, 1):
        where = [jax.random.randint(jax.random.fold_in(own_key, axis), (), 0, length) for axis, length in enumerate(result.shape)]
        where[longest] = (where[longest] + shift) % result.shape[longest]
        spots.append(tuple(where))
    return result.at[spots[0]].set(least).at[spots[1]].set(largest)


def level_of(key, dims, shards, smallest, top_value):
    level = 1.0
    for dim, shards_of in shards:
        steps = jax.random.uniform(jax.random.fold_in(jax.random.fold_in(key, 6), dim), (shards_of,), jnp.float32, smallest / len(shards), top_value / len(shards))
        level = level * jnp.repeat(jnp.exp(steps), dims[dim] // shards_of).reshape((-1,) + (1,) * (len(dims) - 1 - dim))
    return level


def length_profile(amount, total, most, skew):
    portions = [(1 << 20) // math.isqrt(rank ** skew) + 1 for rank in range(2, amount + 1)]
    spare, counts = total - most - (amount - 1), [1] * (amount - 1)
    while spare > 0:
        free = [i for i in range(amount - 1) if counts[i] < most]
        pool, left = sum([portions[i] for i in free]), spare
        for i in free:
            addition = min(most - counts[i], max(1, left * portions[i] // pool), spare)
            counts[i] = counts[i] + addition
            spare = spare - addition
    return np.array([most] + counts)


def uneven(key, count, total, most, lean):
    if count == 2:
        one = jax.random.randint(key, (), max(1, total - most), min(most, total - 1) + 1)
        return jnp.stack([one, total - one])
    tallies = jnp.asarray(length_profile(count, total, most, lean), jnp.int32)
    twos = (count - 1) // 2
    donor, receiver = tallies[1:1 + 2 * twos:2], tallies[2:2 + 2 * twos:2]
    room = jnp.minimum(donor - 1, most - receiver)
    shifted = jax.random.randint(jax.random.fold_in(key, 1), (twos,), 0, 1 << 20) % (room + 1)
    tallies = tallies.at[1:1 + 2 * twos:2].set(donor - shifted).at[2:2 + 2 * twos:2].set(receiver + shifted)
    return tallies[jax.random.permutation(jax.random.fold_in(key, 2), count)]


def assign_block(key, own, number, rows, number_of, top, reach, lean):
    order = jax.random.permutation(key, number_of)
    crowded, usual = load_shares(number_of, rows * top, reach, lean, True), load_shares(number_of, rows * top, reach, lean, False)
    places = jnp.arange(number_of)

    def named(lengths, rotation):
        used = int((lengths > 0).sum())
        fixed = max(1, used // 4)
        passed = fixed + (places - fixed + rotation * (used - fixed)) % max(1, number_of - fixed)
        return jnp.zeros((number_of,), jnp.int32).at[order[jnp.where(places < fixed, places, passed)]].set(jnp.asarray(lengths, jnp.int32))

    lengths = jnp.where(number % 4 == 0, named(crowded, number // 4), named(usual, number - number // 4 - 1))
    mixed = jax.random.permutation(jax.random.fold_in(own, 3), number_of)
    source_of, receiver = mixed[0:number_of // 2 * 2:2], mixed[1:number_of // 2 * 2:2]
    room = jnp.minimum(lengths[source_of] - 1, reach - lengths[receiver]) // 2
    room = jnp.where((source_of == order[0]) | (receiver == order[0]) | (lengths[receiver] == 0), 0, jnp.maximum(room, 0))
    passed = jax.random.randint(jax.random.fold_in(own, 4), (number_of // 2,), 0, 1 << 20) % (room + 1)
    lengths = lengths.at[source_of].add(-passed).at[receiver].add(passed)
    items = jnp.searchsorted(jnp.cumsum(lengths), jnp.arange(rows * top), side="right").astype(jnp.int32)
    listing = items.reshape(top, rows).T
    listing = listing[jax.random.permutation(jax.random.fold_in(own, 1), rows)]
    rotation = jax.random.randint(jax.random.fold_in(own, 2), (rows, 1), 0, top)
    return jnp.take_along_axis(listing, (jnp.arange(top)[None, :] + rotation) % top, axis=1)


def load_shares(amount, total, limit, skew, full):
    loads = [(1 << 20) // math.isqrt(rank ** skew) + 1 for rank in range(1, amount + 1)]
    largest = limit if full else min(limit, max(-(-total // amount), total * loads[0] // sum(loads)))
    least = 1 if total - largest >= amount - 1 else 0
    holding, spare = [largest] + [least] * (amount - 1), total - largest - least * (amount - 1)
    while spare > 0:
        movable = [i for i in range(1, amount) if holding[i] < largest] or [i for i in range(1, amount) if holding[i] < limit]
        pool, remaining = sum([loads[i] for i in movable]), spare
        for i in movable:
            more = min(limit - holding[i], max(1, remaining * loads[i] // pool), spare)
            holding[i] = holding[i] + more
            spare = spare - more
    return np.array(holding)


def scatter_about(own_key, shape, deviation, reach, cuts=(), kind=jnp.bfloat16):
    entries = jax.random.normal(own_key, shape, jnp.float32) * deviation
    if len(cuts) > 0:
        entries = level_of(own_key, shape, cuts, -0.22, 0.18) * entries
    return jnp.clip(entries, min=-reach, max=reach).astype(kind)


def setup_inputs(seed: int = 0, part: int = 0) -> dict:
    key_of = jax.random.split(jax.random.key(seed), 11)
    part_splits = jax.random.split(jax.random.fold_in(key_of[10], part), 11)
    queries = draw_queries(jax.random.fold_in(jax.random.fold_in(key_of[10], part), 71), part)
    key_states = draw_key_states(jax.random.fold_in(jax.random.fold_in(key_of[10], part), 71), part)
    values = scatter_about(part_splits[2], (REQUEST_COUNT, REQUEST_TOKENS, KEY_VALUE_HEADS, HEAD_DIMENSION), 1.0, 6.0, ((0, 2), (1, 4), (2, 2)))
    doc_ids = jax.vmap(lambda own: jnp.searchsorted(jnp.cumsum(uneven(own, DOCS, REQUEST_TOKENS, REQUEST_TOKENS // 2, 0)), jnp.arange(REQUEST_TOKENS), side="right"))(jax.random.split(part_splits[3], REQUEST_COUNT)).reshape((REQUEST_COUNT, REQUEST_TOKENS)).astype(jnp.int32)
    residual = draw_residual(jax.random.fold_in(jax.random.fold_in(key_of[10], part), 71), part)
    out_proj = scatter_about(key_of[5], (QUERY_HEADS * HEAD_DIMENSION, D), (QUERY_HEADS * HEAD_DIMENSION) ** -0.5, 0.125, ((0, 2), (1, 4)))
    norm_gain = jnp.clip(1.0 + 0.1 * jax.random.normal(key_of[6], (D,), jnp.float32), 0.5, 1.5).astype(jnp.bfloat16)
    router = scatter_about(key_of[7], (D, EXPERTS), D ** -0.5, 0.078125, ((1, 2),))
    expert_ids_keys = jax.random.split(jax.random.fold_in(part_splits[8], 1), REQUEST_COUNT * REQUEST_TOKENS // (TOK_DEV // N_TP))
    expert_ids_turns = jax.random.permutation(jax.random.fold_in(part_splits[8], 3), REQUEST_COUNT * REQUEST_TOKENS // (TOK_DEV // N_TP))
    expert_ids = jax.vmap(lambda own, number: assign_block(jax.random.fold_in(part_splits[8], 2), own, number, TOK_DEV // N_TP, EXPERTS, 1, CAP, 2))(expert_ids_keys, expert_ids_turns).reshape((REQUEST_COUNT, REQUEST_TOKENS, 1))
    keep_counts = plant(jax.random.randint(part_splits[9], (EXPERTS,), 1, CAP + 1), jax.random.fold_in(part_splits[9], 1), 1, CAP).astype(jnp.int32)
    return dict(queries=queries, key_states=key_states, values=values, doc_ids=doc_ids, residual=residual, out_proj=out_proj, norm_gain=norm_gain, router=router, expert_ids=expert_ids, keep_counts=keep_counts)


EPSILON = 1e-05

def reference(queries, key_states, values, doc_ids, residual, out_proj, norm_gain, router, expert_ids, keep_counts):
    mixing_ratio = QUERY_HEADS // KEY_VALUE_HEADS
    scale = 1.0 / math.sqrt(HEAD_DIMENSION)
    position = jnp.arange(REQUEST_TOKENS, dtype=jnp.int32)

    def attend_head_group(flattened_index):
        request_number = flattened_index // KEY_VALUE_HEADS
        head_group = flattened_index % KEY_VALUE_HEADS
        query_rows = lax.dynamic_index_in_dim(queries, request_number, 0, False)
        query_rows = lax.dynamic_slice_in_dim(query_rows, head_group * mixing_ratio, mixing_ratio, 1)
        key_rows = lax.dynamic_index_in_dim(lax.dynamic_index_in_dim(key_states, request_number, 0, False), head_group, 1, False)
        value_rows = lax.dynamic_index_in_dim(lax.dynamic_index_in_dim(values, request_number, 0, False), head_group, 1, False)
        documents = lax.dynamic_index_in_dim(doc_ids, request_number, 0, False)
        scores = jnp.einsum('qrd,kd->rqk', query_rows.astype(jnp.float32), key_rows.astype(jnp.float32)) * scale
        allowed = (position[None, :] <= position[:, None]) & (documents[None, :] == documents[:, None])
        masked = jnp.where(allowed[None], scores, -jnp.inf)
        highest = lax.optimization_barrier(jnp.max(masked, axis=2, keepdims=True))
        weights = jnp.where(allowed[None], jnp.exp(scores - highest), 0.0)
        totals = lax.optimization_barrier(jnp.sum(weights, axis=2, keepdims=True))
        rounded = weights.astype(jnp.bfloat16).astype(jnp.float32)
        summed = jnp.einsum('rqk,kd->rqd', rounded, value_rows.astype(jnp.float32))
        return (summed / totals).astype(jnp.bfloat16)
    head_list = lax.map(attend_head_group, jnp.arange(REQUEST_COUNT * KEY_VALUE_HEADS, dtype=jnp.int32))
    blended_output = head_list.reshape(REQUEST_COUNT, KEY_VALUE_HEADS, mixing_ratio, REQUEST_TOKENS, HEAD_DIMENSION).transpose(0, 3, 1, 2, 4).reshape(REQUEST_COUNT * REQUEST_TOKENS, QUERY_HEADS * HEAD_DIMENSION)
    projected = jnp.dot(blended_output, out_proj, preferred_element_type=jnp.float32).reshape(REQUEST_COUNT, REQUEST_TOKENS, D)
    hidden = residual.astype(jnp.float32) + projected
    power = lax.optimization_barrier(jnp.mean(hidden * hidden, axis=2, keepdims=True))
    normed = (hidden * lax.rsqrt(power + EPSILON) * norm_gain.astype(jnp.float32)).astype(jnp.bfloat16)
    blocks = N_CTX * N_TP
    block_rows = TOK_DEV // N_TP
    normed_blocks = normed.reshape(REQUEST_COUNT, blocks, block_rows, D)
    id_blocks = expert_ids.reshape(REQUEST_COUNT, blocks, block_rows)
    expert_iota = jnp.arange(EXPERTS, dtype=jnp.int32)
    slot_iota = jnp.arange(EXPERTS * CAP, dtype=jnp.int32)
    router_wide = router.astype(jnp.float32)

    def route_block(flattened_index):
        block = flattened_index // REQUEST_COUNT
        request_number = flattened_index % REQUEST_COUNT
        token_rows = lax.dynamic_index_in_dim(lax.dynamic_index_in_dim(normed_blocks, request_number, 0, False), block, 0, False)
        chosen = lax.dynamic_index_in_dim(lax.dynamic_index_in_dim(id_blocks, request_number, 0, False), block, 0, False)
        onehot = (chosen[:, None] == expert_iota[None, :]).astype(jnp.int32)
        earlier = jnp.cumsum(onehot, axis=0) - onehot
        ranking = lax.optimization_barrier(jnp.sum(onehot * earlier, axis=1))
        limits = lax.optimization_barrier(jnp.sum(onehot * keep_counts[None, :], axis=1))
        kept = ranking < limits
        target = chosen * CAP + ranking
        table = (slot_iota[:, None] == target[None, :]) & kept[None, :]
        slots = jnp.dot(table.astype(jnp.bfloat16), token_rows, preferred_element_type=jnp.float32)
        slots = slots.astype(jnp.bfloat16).astype(jnp.float32).reshape(EXPERTS, CAP, D)
        logits = jnp.einsum('ecd,de->ec', slots, router_wide)
        return (slots * jax.nn.sigmoid(logits)[..., None]).astype(jnp.bfloat16)
    return lax.map(route_block, jnp.arange(blocks * REQUEST_COUNT, dtype=jnp.int32))
```

```python
import functools
import math

import jax
import jax.numpy as jnp
from jax import lax
from jax.experimental import pallas as pl
from jax.experimental.pallas import tpu as pltpu
from jax.sharding import PartitionSpec as P

CAP = 2
EPSILON = 1e-05
MESH = pl.DeviceIdType.MESH


def kernel(
    sizes,
    q_ref,
    kv_ref,
    doc_ref,
    residual_hbm,
    weight_hbm,
    gain_ref,
    router_ref,
    ids_ref,
    keep_ref,
    out_ref,
    kv_in,
    doc_in,
    attn,
    weight,
    residual,
    product,
    part_out,
    part_in,
    res_out,
    res_in,
    slot_out,
    slot_in,
    load_sem,
    kv_send,
    kv_recv,
    doc_send,
    doc_recv,
    right_send,
    left_send,
    attn_recv,
    part_send,
    part_recv,
    res_send,
    res_recv,
    slot_send,
    slot_recv,
):
    ctx_count, exp_count, back = sizes
    heads, tokens, size = q_ref.shape
    groups = kv_ref.shape[0]
    ratio = heads // groups
    half = tokens // 2
    columns = weight.shape[1]
    depth = weight.shape[0] // groups
    slots = slot_in.shape[2]
    me = lax.axis_index("ctx")
    mine = lax.axis_index("exp")
    core = lax.axis_index("tp")

    load_weight = pltpu.make_async_copy(weight_hbm, weight, load_sem.at[0])
    load_weight.start()
    aligned = columns % 128 == 0
    load_residual = []
    for block in range(ctx_count):
        there = slice(block * columns, (block + 1) * columns)
        load_residual.append(
            pltpu.make_async_copy(
                residual_hbm.at[:, there] if aligned else residual_hbm.at[block],
                residual.at[block],
                load_sem.at[1 + block],
            )
        )
        load_residual[-1].start()

    barrier = pltpu.get_barrier_semaphore()
    for shift in range(1, ctx_count):
        pl.semaphore_signal(
            barrier,
            inc=1,
            device_id={"ctx": lax.rem(me + shift, ctx_count)},
            device_id_type=MESH,
        )
    for shift in range(1, exp_count):
        pl.semaphore_signal(
            barrier,
            inc=1,
            device_id={"exp": lax.rem(mine + shift, exp_count)},
            device_id_type=MESH,
        )
    pl.semaphore_signal(barrier, inc=1, device_id={"tp": 1 - core}, device_id_type=MESH)

    row = lax.broadcasted_iota(jnp.int32, (half, half), 0)
    lane = lax.broadcasted_iota(jnp.int32, (half, half), 1)
    ids_row = ids_ref[...]
    ids_column = jnp.sum(jnp.where(row == lane, ids_row, 0), axis=1, keepdims=True)
    ranking = jnp.sum(
        jnp.where((ids_column == ids_row) & (row < lane), 1, 0), axis=0, keepdims=True
    )
    experts = keep_ref.shape[1]
    square_row = lax.broadcasted_iota(jnp.int32, (experts, experts), 0)
    square_lane = lax.broadcasted_iota(jnp.int32, (experts, experts), 1)
    keep_column = jnp.sum(
        jnp.where(square_row == square_lane, keep_ref[...], 0), axis=1, keepdims=True
    )
    expert_row = lax.broadcasted_iota(jnp.int32, (experts, half), 0)
    limits = jnp.sum(jnp.where(expert_row == ids_row, keep_column, 0), axis=0, keepdims=True)
    target = jnp.where(ranking < limits, ids_row * CAP + ranking, -1)
    slot_row = lax.broadcasted_iota(jnp.int32, (slots, half), 0)

    pl.semaphore_wait(barrier, ctx_count + exp_count - 1)

    def kv_copy(group, shift):
        return pltpu.make_async_remote_copy(
            src_ref=kv_ref.at[group],
            dst_ref=kv_in.at[group, shift - 1],
            send_sem=kv_send.at[group, shift - 1],
            recv_sem=kv_recv.at[group, shift - 1],
            device_id={"ctx": lax.rem(me + shift, ctx_count)},
            device_id_type=MESH,
        )

    def doc_copy(shift):
        return pltpu.make_async_remote_copy(
            src_ref=doc_ref,
            dst_ref=doc_in.at[shift - 1],
            send_sem=doc_send.at[shift - 1],
            recv_sem=doc_recv.at[shift - 1],
            device_id={"ctx": lax.rem(me + shift, ctx_count)},
            device_id_type=MESH,
        )

    for shift in range(1, back + 1):

        @pl.when(me + shift < ctx_count)
        def _(shift=shift):
            doc_copy(shift).start()

    for group in range(groups):
        for shift in range(1, back + 1):

            @pl.when(me + shift < ctx_count)
            def _(group=group, shift=shift):
                kv_copy(group, shift).start()

    for shift in range(1, back + 1):

        @pl.when(me < shift)
        def _(shift=shift):
            doc_in[shift - 1] = jnp.full(doc_in.shape[1:], -1, jnp.int32)
            for group in range(groups):
                kv_in[group, shift - 1] = jnp.zeros(kv_in.shape[2:], kv_in.dtype)

        @pl.when(me >= shift)
        def _(shift=shift):
            doc_copy(shift).wait_recv()

    square = lax.broadcasted_iota(jnp.int32, (tokens, tokens), 0)
    across = lax.broadcasted_iota(jnp.int32, (tokens, tokens), 1)
    doc_row = doc_ref[...]
    doc_column = jnp.sum(jnp.where(square == across, doc_row, 0), axis=1, keepdims=True)
    allowed = [(across <= square) & (doc_row == doc_column)]
    for shift in range(1, back + 1):
        allowed.append(doc_in[shift - 1] == doc_column)
    allowed = jnp.concatenate(
        [jnp.where(piece, 1.0, 0.0) for piece in allowed], axis=1
    )
    allowed = allowed > 0.5
    scale = 1.0 / math.sqrt(size)

    def attn_copy(block, group, rightward):
        to = me + 1 if rightward else me - 1
        sends = right_send if rightward else left_send
        return pltpu.make_async_remote_copy(
            src_ref=attn.at[block, group],
            dst_ref=attn.at[block, group],
            send_sem=sends.at[block, group],
            recv_sem=attn_recv.at[block, group],
            device_id={"ctx": lax.rem(to + ctx_count, ctx_count)},
            device_id_type=MESH,
        )

    for group in range(groups):
        for shift in range(1, back + 1):

            @pl.when(me >= shift)
            def _(group=group, shift=shift):
                kv_copy(group, shift).wait_recv()

        keys = jnp.concatenate(
            [kv_ref[group, 0]] + [kv_in[group, shift, 0] for shift in range(back)], axis=0
        )
        vals = jnp.concatenate(
            [kv_ref[group, 1]] + [kv_in[group, shift, 1] for shift in range(back)], axis=0
        )
        for head in range(ratio):
            scores = (
                lax.dot_general(
                    q_ref[group * ratio + head],
                    keys,
                    (((1,), (1,)), ((), ())),
                    preferred_element_type=jnp.float32,
                )
                * scale
            )
            masked = jnp.where(allowed, scores, -1e30)
            highest = jnp.max(masked, axis=1, keepdims=True)
            weights = jnp.where(allowed, jnp.exp(masked - highest), 0.0)
            totals = jnp.sum(weights, axis=1, keepdims=True)
            mixed = jnp.dot(weights.astype(jnp.bfloat16), vals, preferred_element_type=jnp.float32)
            attn[me, group, :, head * size : (head + 1) * size] = (mixed / totals).astype(
                jnp.bfloat16
            )

        @pl.when(me < ctx_count - 1)
        def _(group=group):
            attn_copy(me, group, True).start()

        @pl.when(me > 0)
        def _(group=group):
            attn_copy(me, group, False).start()

    def part_copy(block):
        return pltpu.make_async_remote_copy(
            src_ref=part_out.at[block],
            dst_ref=part_in.at[block],
            send_sem=part_send.at[block],
            recv_sem=part_recv.at[block],
            device_id={"tp": 1 - core},
            device_id_type=MESH,
        )

    def res_copy(block, peer):
        return pltpu.make_async_remote_copy(
            src_ref=res_out.at[block],
            dst_ref=res_in.at[me],
            send_sem=res_send.at[block],
            recv_sem=res_recv.at[peer],
            device_id={"ctx": block},
            device_id_type=MESH,
        )

    def slot_copy(shift, block, peer):
        return pltpu.make_async_remote_copy(
            src_ref=slot_out.at[shift - 1, block],
            dst_ref=slot_in.at[mine, block],
            send_sem=slot_send.at[shift - 1, block],
            recv_sem=slot_recv.at[peer, block],
            device_id={"exp": lax.rem(mine + shift, exp_count)},
            device_id_type=MESH,
        )

    tile = math.gcd(columns, 256)

    def project(block):
        for first in range(0, columns, tile):
            total = None
            for group in range(groups):
                term = jnp.dot(
                    attn[block, group],
                    weight[group * depth : (group + 1) * depth, first : first + tile],
                    preferred_element_type=jnp.float32,
                )
                total = term if total is None else total + term
            product[block, 0, :, first : first + tile] = total[:half]
            product[block, 1, :, first : first + tile] = total[half:]
        part_out[block] = product[block, 1 - core].astype(jnp.bfloat16)
        part_copy(block).start()

    def finish(block):
        part_copy(block).wait_recv()
        return (product[block, core] + part_in[block].astype(jnp.float32)).astype(jnp.bfloat16)

    def place(block):
        hidden = (
            residual[block].astype(jnp.float32)
            + res_in[block].astype(jnp.float32)
        ).astype(jnp.bfloat16)
        for shift in range(exp_count):
            peer = lax.rem(mine + shift, exp_count)
            table = (slot_row + peer * slots == target).astype(jnp.bfloat16)
            chosen = jnp.dot(table, hidden, preferred_element_type=jnp.float32).astype(
                jnp.bfloat16
            )
            if shift == 0:
                slot_in[mine, block] = chosen
            else:
                slot_out[shift - 1, block] = chosen
                slot_copy(shift, block, mine).start()

    load_weight.wait()
    project(me)
    for load in load_residual:
        load.wait()
    res_in[me] = finish(me)
    place(me)

    def step(distance, carry):
        left, right = me - distance, me + distance
        inside = distance < ctx_count
        has_left = (left >= 0) & inside
        has_right = (right < ctx_count) & inside

        @pl.when(has_left)
        def _():
            for group in range(groups):
                attn_copy(left, group, True).wait_recv()

                @pl.when(me < ctx_count - 1)
                def _():
                    attn_copy(left, group, True).start()

        @pl.when(has_right)
        def _():
            for group in range(groups):
                attn_copy(right, group, False).wait_recv()

                @pl.when(me > 0)
                def _():
                    attn_copy(right, group, False).start()

        for block, has in ((left, has_left), (right, has_right)):

            @pl.when(has)
            def _(block=block):
                project(block)

        for block, has in ((left, has_left), (right, has_right)):

            @pl.when(has)
            def _(block=block):
                res_out[block] = finish(block)
                res_copy(block, me).start()

        for block, ok in (
            (left + 1, (left + 1 >= 0) & (distance >= 2)),
            (right - 1, (right - 1 < ctx_count) & (distance >= 2)),
        ):

            @pl.when(ok)
            def _(block=block):
                res_copy(me, block).wait_recv()
                place(block)

        return carry

    lax.fori_loop(1, ctx_count + 1, step, 0)

    spread = lax.broadcasted_iota(jnp.int32, (slots, router_ref.shape[0]), 0) // CAP
    expert = lax.broadcasted_iota(jnp.int32, (slots, router_ref.shape[0]), 1)
    for shift in range(exp_count):
        peer = lax.rem(mine + shift, exp_count)
        if shift:
            for block in range(ctx_count):
                slot_copy(1, block, peer).wait_recv()
        power = 0.0
        for block in range(ctx_count):
            hidden = slot_in[peer, block].astype(jnp.float32)
            power = power + jnp.sum(hidden * hidden, axis=1, keepdims=True)
        factor = lax.rsqrt(power / (columns * ctx_count) + EPSILON)
        logits = 0.0
        for block in range(ctx_count):
            there = slice(block * columns, (block + 1) * columns)
            normed = (
                slot_in[peer, block].astype(jnp.float32)
                * factor
                * gain_ref[:, there].astype(jnp.float32)
            ).astype(jnp.bfloat16)
            slot_in[peer, block] = normed
            logits = logits + lax.dot_general(
                normed,
                router_ref[:, there],
                (((1,), (1,)), ((), ())),
                preferred_element_type=jnp.float32,
            )
        logit = jnp.sum(jnp.where(spread == expert, logits, 0.0), axis=1, keepdims=True)
        gate = jax.nn.sigmoid(logit)
        for block in range(ctx_count):
            out_ref[peer, :, block * columns : (block + 1) * columns] = (
                slot_in[peer, block].astype(jnp.float32) * gate
            ).astype(jnp.bfloat16)

    for shift in range(1, back + 1):

        @pl.when(me + shift < ctx_count)
        def _(shift=shift):
            doc_copy(shift).wait_send()
            for group in range(groups):
                kv_copy(group, shift).wait_send()

    def drain(block, carry):
        part_copy(block).wait_send()
        for shift in range(1, exp_count):
            slot_copy(shift, block, mine).wait_send()

        @pl.when(block != me)
        def _():
            res_copy(block, me).wait_send()

        for group in range(groups):

            @pl.when((block <= me) & (me < ctx_count - 1))
            def _(group=group):
                attn_copy(block, group, True).wait_send()

            @pl.when((block >= me) & (me > 0))
            def _(group=group):
                attn_copy(block, group, False).wait_send()

        return carry

    lax.fori_loop(0, ctx_count, drain, 0)


def on_device(
    queries,
    key_states,
    values,
    doc_ids,
    residual,
    out_proj,
    norm_gain,
    router,
    expert_ids,
    keep_counts,
):
    tokens, heads, size = queries.shape[1:]
    groups = key_states.shape[2]
    ctx_count = lax.axis_size("ctx")
    exp_count = lax.axis_size("exp")
    features, columns = out_proj.shape
    half = residual.shape[1]
    width = residual.shape[2]
    experts = keep_counts.shape[0]
    slots = experts // exp_count * CAP
    longest = tokens * ctx_count // 2
    back = min(ctx_count - 1, -(-(longest - 1) // tokens))
    kv = jnp.stack([key_states[0], values[0]]).transpose(2, 0, 1, 3)
    vmem = pl.BlockSpec(memory_space=pltpu.VMEM)
    hbm = pl.BlockSpec(memory_space=pl.ANY)
    bf16, f32 = jnp.bfloat16, jnp.float32
    dma = pltpu.SemaphoreType.DMA
    n = ctx_count
    stream = residual[0]
    if columns % 128:
        stream = stream.reshape(half, ctx_count, columns).transpose(1, 0, 2)
    out = pl.pallas_call(
        functools.partial(kernel, (ctx_count, exp_count, back)),
        out_shape=jax.ShapeDtypeStruct((exp_count, slots, width), bf16),
        in_specs=[vmem, vmem, vmem, hbm, hbm, vmem, vmem, vmem, vmem],
        out_specs=vmem,
        scratch_shapes=[
            pltpu.VMEM((groups, back, 2, tokens, size), bf16),
            pltpu.VMEM((back, 1, tokens), jnp.int32),
            pltpu.VMEM((n, groups, tokens, features // groups), bf16),
            pltpu.VMEM((features, columns), bf16),
            pltpu.VMEM((n, half, columns), bf16),
            pltpu.VMEM((n, 2, half, columns), f32),
            pltpu.VMEM((n, half, columns), bf16),
            pltpu.VMEM((n, half, columns), bf16),
            pltpu.VMEM((n, half, columns), bf16),
            pltpu.VMEM((n, half, columns), bf16),
            pltpu.VMEM((exp_count - 1, n, slots, columns), bf16),
            pltpu.VMEM((exp_count, n, slots, columns), bf16),
            dma((1 + n,)),
            dma((groups, back)),
            dma((groups, back)),
            dma((back,)),
            dma((back,)),
            dma((n, groups)),
            dma((n, groups)),
            dma((n, groups)),
            dma((n,)),
            dma((n,)),
            dma((n,)),
            dma((n,)),
            dma((exp_count - 1, n)),
            dma((exp_count, n)),
        ],
        compiler_params=pltpu.CompilerParams(collective_id=0, has_side_effects=True),
    )(
        queries[0].transpose(1, 0, 2),
        kv,
        doc_ids,
        stream,
        out_proj,
        norm_gain.reshape(1, width),
        router.T,
        expert_ids.reshape(1, half),
        keep_counts.reshape(1, experts),
    )
    return out.reshape(exp_count, experts // exp_count, CAP, width)


def solution(mesh):
    placed = (
        P(("groups", "exp"), "ctx", "tp", None),
        P(("groups", "exp"), "ctx", "tp", None),
        P(("groups", "exp"), "ctx", "tp", None),
        P(("groups", "exp"), "ctx"),
        P(("groups", "exp"), ("ctx", "tp"), None),
        P("tp", "ctx"),
        P(),
        P(None, "exp"),
        P(("groups", "exp"), ("ctx", "tp"), None),
        P("groups"),
    )
    return jax.shard_map(
        on_device,
        mesh=mesh,
        in_specs=placed,
        out_specs=P(("groups", "ctx", "tp"), "exp", None, None),
        check_vma=False,
    )
```

```python
import functools
import math

import jax
import jax.numpy as jnp
from jax import lax
from jax.experimental import pallas as pl
from jax.experimental.pallas import tpu as pltpu
from jax.sharding import PartitionSpec as P

CAP = 2
EPSILON = 1e-05
MESH = pl.DeviceIdType.MESH


def kernel(
    sizes,
    q_ref,
    key_ref,
    value_ref,
    doc_ref,
    residual_hbm,
    weight_hbm,
    gain_ref,
    router_ref,
    ids_ref,
    keep_ref,
    out_ref,
    kv_out,
    kv_in,
    gain,
    tally,
    doc_in,
    attn,
    weight,
    residual,
    product,
    part_out,
    part_in,
    res_out,
    res_in,
    slot_out,
    slot_in,
    load_sem,
    kv_send,
    kv_recv,
    doc_send,
    doc_recv,
    right_send,
    left_send,
    attn_recv,
    part_send,
    part_recv,
    res_send,
    res_recv,
    slot_send,
    slot_recv,
):
    ctx_count, exp_count, back, pieces = sizes
    heads, tokens, size = q_ref.shape
    groups = kv_out.shape[0]
    ratio = heads // groups
    half = tokens // 2
    columns = weight.shape[1]
    depth = weight.shape[0] // groups
    slots = slot_in.shape[3]
    part = columns // pieces
    me = lax.axis_index("ctx")
    mine = lax.axis_index("exp")
    core = lax.axis_index("tp")

    load_weight = pltpu.make_async_copy(weight_hbm, weight, load_sem.at[0])
    load_weight.start()
    aligned = columns % 128 == 0
    load_residual = []
    for block in range(ctx_count):
        there = slice(block * columns, (block + 1) * columns)
        load_residual.append(
            pltpu.make_async_copy(
                residual_hbm.at[:, there] if aligned else residual_hbm.at[block],
                residual.at[block],
                load_sem.at[1 + block],
            )
        )
        load_residual[-1].start()

    barrier = pltpu.get_barrier_semaphore()
    for shift in range(1, ctx_count):
        pl.semaphore_signal(
            barrier,
            inc=1,
            device_id={"ctx": lax.rem(me + shift, ctx_count)},
            device_id_type=MESH,
        )
    for shift in range(1, exp_count):
        pl.semaphore_signal(
            barrier,
            inc=1,
            device_id={"exp": lax.rem(mine + shift, exp_count)},
            device_id_type=MESH,
        )
    pl.semaphore_signal(barrier, inc=1, device_id={"tp": 1 - core}, device_id_type=MESH)

    for group in range(groups):
        kv_out[group, 0] = key_ref[:, group, :]
        kv_out[group, 1] = value_ref[:, group, :]

    pl.semaphore_wait(barrier, ctx_count + exp_count - 1)

    def kv_copy(group, shift):
        return pltpu.make_async_remote_copy(
            src_ref=kv_out.at[group] if shift == 1 else kv_in.at[group, shift - 2],
            dst_ref=kv_in.at[group, shift - 1],
            send_sem=kv_send.at[group, shift - 1],
            recv_sem=kv_recv.at[group, shift - 1],
            device_id={"ctx": lax.rem(me + 1, ctx_count)},
            device_id_type=MESH,
        )

    def doc_copy(shift):
        return pltpu.make_async_remote_copy(
            src_ref=doc_ref,
            dst_ref=doc_in.at[shift - 1],
            send_sem=doc_send.at[shift - 1],
            recv_sem=doc_recv.at[shift - 1],
            device_id={"ctx": lax.rem(me + shift, ctx_count)},
            device_id_type=MESH,
        )

    for shift in range(1, back + 1):

        @pl.when(me + shift < ctx_count)
        def _(shift=shift):
            doc_copy(shift).start()

    for group in range(groups):

        @pl.when(me + 1 < ctx_count)
        def _(group=group):
            kv_copy(group, 1).start()

    row = lax.broadcasted_iota(jnp.int32, (half, half), 0)
    lane = lax.broadcasted_iota(jnp.int32, (half, half), 1)
    ids_row = ids_ref[...]
    ids_column = jnp.sum(jnp.where(row == lane, ids_row, 0), axis=1, keepdims=True)
    ranking = jnp.sum(
        jnp.where((ids_column == ids_row) & (row < lane), 1, 0), axis=0, keepdims=True
    )
    experts = keep_ref.shape[1]
    square_row = lax.broadcasted_iota(jnp.int32, (experts, experts), 0)
    square_lane = lax.broadcasted_iota(jnp.int32, (experts, experts), 1)
    keep_column = jnp.sum(
        jnp.where(square_row == square_lane, keep_ref[...], 0), axis=1, keepdims=True
    )
    expert_row = lax.broadcasted_iota(jnp.int32, (experts, half), 0)
    limits = jnp.sum(jnp.where(expert_row == ids_row, keep_column, 0), axis=0, keepdims=True)
    target = jnp.where(ranking < limits, ids_row * CAP + ranking, -1)
    slot_row = lax.broadcasted_iota(jnp.int32, (slots, half), 0)

    wide = gain_ref[...].astype(jnp.float32)
    for line in range(wide.shape[0]):
        gain[:, line * 128 : (line + 1) * 128] = wide[line : line + 1]

    for shift in range(1, back + 1):

        @pl.when(me < shift)
        def _(shift=shift):
            doc_in[shift - 1] = jnp.full(doc_in.shape[1:], -1, jnp.int32)
            for group in range(groups):
                kv_in[group, shift - 1] = jnp.zeros(kv_in.shape[2:], kv_in.dtype)

        @pl.when(me >= shift)
        def _(shift=shift):
            doc_copy(shift).wait_recv()

    square = lax.broadcasted_iota(jnp.int32, (tokens, tokens), 0)
    across = lax.broadcasted_iota(jnp.int32, (tokens, tokens), 1)
    doc_row = doc_ref[...]
    doc_column = jnp.sum(jnp.where(square == across, doc_row, 0), axis=1, keepdims=True)
    allowed = [(across <= square) & (doc_row == doc_column)]
    for shift in range(1, back + 1):
        allowed.append(doc_in[shift - 1] == doc_column)
    allowed = jnp.concatenate(
        [jnp.where(piece, 1.0, 0.0) for piece in allowed], axis=1
    )
    allowed = allowed > 0.5
    scale = 1.0 / math.sqrt(size)

    def attn_copy(block, group, rightward):
        to = me + 1 if rightward else me - 1
        sends = right_send if rightward else left_send
        return pltpu.make_async_remote_copy(
            src_ref=attn.at[block, group],
            dst_ref=attn.at[block, group],
            send_sem=sends.at[block, group],
            recv_sem=attn_recv.at[block, group],
            device_id={"ctx": lax.rem(to + ctx_count, ctx_count)},
            device_id_type=MESH,
        )

    for group in range(groups):
        for shift in range(1, back + 1):

            @pl.when(me >= shift)
            def _(group=group, shift=shift):
                kv_copy(group, shift).wait_recv()
                if shift < back:

                    @pl.when(me + 1 < ctx_count)
                    def _():
                        kv_copy(group, shift + 1).start()

        keys = jnp.concatenate(
            [kv_out[group, 0]] + [kv_in[group, shift, 0] for shift in range(back)], axis=0
        )
        vals = jnp.concatenate(
            [kv_out[group, 1]] + [kv_in[group, shift, 1] for shift in range(back)], axis=0
        )
        for head in range(ratio):
            scores = (
                lax.dot_general(
                    q_ref[group * ratio + head],
                    keys,
                    (((1,), (1,)), ((), ())),
                    preferred_element_type=jnp.float32,
                )
                * scale
            )
            masked = jnp.where(allowed, scores, -1e30)
            highest = jnp.max(masked, axis=1, keepdims=True)
            weights = jnp.where(allowed, jnp.exp(masked - highest), 0.0)
            totals = jnp.sum(weights, axis=1, keepdims=True)
            mixed = jnp.dot(weights.astype(jnp.bfloat16), vals, preferred_element_type=jnp.float32)
            attn[me, group, :, head * size : (head + 1) * size] = (mixed / totals).astype(
                jnp.bfloat16
            )

        @pl.when(me < ctx_count - 1)
        def _(group=group):
            attn_copy(me, group, True).start()

        @pl.when(me > 0)
        def _(group=group):
            attn_copy(me, group, False).start()

    def part_copy(block, piece):
        return pltpu.make_async_remote_copy(
            src_ref=part_out.at[block, piece],
            dst_ref=part_in.at[block, piece],
            send_sem=part_send.at[block, piece],
            recv_sem=part_recv.at[block, piece],
            device_id={"tp": 1 - core},
            device_id_type=MESH,
        )

    def res_copy(block, peer, piece):
        return pltpu.make_async_remote_copy(
            src_ref=res_out.at[block, piece],
            dst_ref=res_in.at[me, piece],
            send_sem=res_send.at[block, piece],
            recv_sem=res_recv.at[peer, piece],
            device_id={"ctx": block},
            device_id_type=MESH,
        )

    def slot_copy(shift, block, peer, piece):
        return pltpu.make_async_remote_copy(
            src_ref=slot_out.at[shift - 1, block, piece],
            dst_ref=slot_in.at[mine, block, piece],
            send_sem=slot_send.at[shift - 1, block, piece],
            recv_sem=slot_recv.at[peer, block, piece],
            device_id={"exp": lax.rem(mine + shift, exp_count)},
            device_id_type=MESH,
        )

    tile = math.gcd(part, 128)

    def project(block, piece):
        for first in range(0, part, tile):
            there = slice(piece * part + first, piece * part + first + tile)
            total = None
            for group in range(groups):
                term = jnp.dot(
                    attn[block, group],
                    weight[group * depth : (group + 1) * depth, there],
                    preferred_element_type=jnp.float32,
                )
                total = term if total is None else total + term
            product[block, piece, 0, :, first : first + tile] = total[:half]
            product[block, piece, 1, :, first : first + tile] = total[half:]
        part_out[block, piece] = product[block, piece, 1 - core].astype(jnp.bfloat16)
        part_copy(block, piece).start()

    def finish(block, piece):
        part_copy(block, piece).wait_recv()
        return (
            product[block, piece, core] + part_in[block, piece].astype(jnp.float32)
        ).astype(jnp.bfloat16)

    def place(block, piece):
        hidden = (
            residual[block, :, piece * part : (piece + 1) * part].astype(jnp.float32)
            + res_in[block, piece].astype(jnp.float32)
        ).astype(jnp.bfloat16)
        for shift in (*range(1, exp_count), 0):
            peer = lax.rem(mine + shift, exp_count)
            table = (slot_row + peer * slots == target).astype(jnp.bfloat16)
            chosen = jnp.dot(table, hidden, preferred_element_type=jnp.float32).astype(
                jnp.bfloat16
            )
            if shift == 0:
                slot_in[mine, block, piece] = chosen
            else:
                slot_out[shift - 1, block, piece] = chosen
                slot_copy(shift, block, mine, piece).start()

    load_weight.wait()
    for piece in range(pieces):
        project(me, piece)
    for load in load_residual:
        load.wait()
    for piece in range(pieces):
        res_in[me, piece] = finish(me, piece)
        place(me, piece)

    def step(distance, carry):
        left, right = me - distance, me + distance
        inside = distance < ctx_count
        has_left = (left >= 0) & inside
        has_right = (right < ctx_count) & inside

        @pl.when(has_left)
        def _():
            for group in range(groups):
                attn_copy(left, group, True).wait_recv()

                @pl.when(me < ctx_count - 1)
                def _():
                    attn_copy(left, group, True).start()

        @pl.when(has_right)
        def _():
            for group in range(groups):
                attn_copy(right, group, False).wait_recv()

                @pl.when(me > 0)
                def _():
                    attn_copy(right, group, False).start()

        for piece in range(pieces):
            for block, has in ((left, has_left), (right, has_right)):

                @pl.when(has)
                def _(block=block):
                    project(block, piece)

        for piece in range(pieces):
            for block, has in ((left, has_left), (right, has_right)):

                @pl.when(has)
                def _(block=block):
                    res_out[block, piece] = finish(block, piece)
                    res_copy(block, me, piece).start()

        for piece in range(pieces):
            for block, ok in (
                (left + 1, (left + 1 >= 0) & (distance >= 2)),
                (right - 1, (right - 1 < ctx_count) & (distance >= 2)),
            ):

                @pl.when(ok)
                def _(block=block):
                    res_copy(me, block, piece).wait_recv()
                    place(block, piece)

        return carry

    lax.fori_loop(1, ctx_count + 1, step, 0)

    spread = lax.broadcasted_iota(jnp.int32, (slots, router_ref.shape[0]), 0) // CAP
    expert = lax.broadcasted_iota(jnp.int32, (slots, router_ref.shape[0]), 1)
    for shift in range(exp_count):
        peer = lax.rem(mine + shift, exp_count)
        tally[...] = jnp.zeros_like(tally)

        def absorb(block):
            for piece in range(pieces):
                if shift:
                    slot_copy(1, block, peer, piece).wait_recv()
                hidden = slot_in[peer, block, piece].astype(jnp.float32)
                tally[:, :1] += jnp.sum(hidden * hidden, axis=1, keepdims=True)

        absorb(me)

        def gather(distance, carry):
            @pl.when(me >= distance)
            def _():
                absorb(me - distance)

            @pl.when(me + distance < ctx_count)
            def _():
                absorb(me + distance)

            return carry

        lax.fori_loop(1, ctx_count, gather, 0)
        factor = lax.rsqrt(tally[:, :1] / (columns * ctx_count) + EPSILON)
        logits = 0.0
        for block in range(ctx_count):
            for piece in range(pieces):
                first = block * columns + piece * part
                there = slice(first, first + part)
                normed = (
                    slot_in[peer, block, piece].astype(jnp.float32) * factor * gain[:, there]
                ).astype(jnp.bfloat16)
                slot_in[peer, block, piece] = normed
                logits = logits + lax.dot_general(
                    normed,
                    router_ref[:, there],
                    (((1,), (1,)), ((), ())),
                    preferred_element_type=jnp.float32,
                )
        logit = jnp.sum(jnp.where(spread == expert, logits, 0.0), axis=1, keepdims=True)
        gate = jax.nn.sigmoid(logit)
        for block in range(ctx_count):
            for piece in range(pieces):
                first = block * columns + piece * part
                done = slot_in[peer, block, piece].astype(jnp.float32) * gate
                out_ref[peer, :, :, first : first + part] = done.reshape(
                    slots // CAP, CAP, part
                ).astype(jnp.bfloat16)

    for shift in range(1, back + 1):

        @pl.when(me + shift < ctx_count)
        def _(shift=shift):
            doc_copy(shift).wait_send()

        @pl.when((me + 1 < ctx_count) & (me + 1 >= shift))
        def _(shift=shift):
            for group in range(groups):
                kv_copy(group, shift).wait_send()

    def drain(block, carry):
        for piece in range(pieces):
            part_copy(block, piece).wait_send()
            for shift in range(1, exp_count):
                slot_copy(shift, block, mine, piece).wait_send()

        @pl.when(block != me)
        def _():
            for piece in range(pieces):
                res_copy(block, me, piece).wait_send()

        for group in range(groups):

            @pl.when((block <= me) & (me < ctx_count - 1))
            def _(group=group):
                attn_copy(block, group, True).wait_send()

            @pl.when((block >= me) & (me > 0))
            def _(group=group):
                attn_copy(block, group, False).wait_send()

        return carry

    lax.fori_loop(0, ctx_count, drain, 0)


def on_device(
    queries,
    key_states,
    values,
    doc_ids,
    residual,
    out_proj,
    norm_gain,
    router,
    expert_ids,
    keep_counts,
):
    tokens, heads, size = queries.shape[1:]
    groups = key_states.shape[2]
    ctx_count = lax.axis_size("ctx")
    exp_count = lax.axis_size("exp")
    features, columns = out_proj.shape
    half = residual.shape[1]
    width = residual.shape[2]
    experts = keep_counts.shape[0]
    slots = experts // exp_count * CAP
    longest = tokens * ctx_count // 2
    back = min(ctx_count - 1, -(-(longest - 1) // tokens))
    pieces = 2
    part = columns // pieces
    vmem = pl.BlockSpec(memory_space=pltpu.VMEM)
    hbm = pl.BlockSpec(memory_space=pl.ANY)
    bf16, f32 = jnp.bfloat16, jnp.float32
    dma = pltpu.SemaphoreType.DMA
    n = ctx_count
    stream = residual[0]
    if columns % 128:
        stream = stream.reshape(half, ctx_count, columns).transpose(1, 0, 2)
    out = pl.pallas_call(
        functools.partial(kernel, (ctx_count, exp_count, back, pieces)),
        out_shape=jax.ShapeDtypeStruct((exp_count, slots // CAP, CAP, width), bf16),
        in_specs=[vmem, vmem, vmem, vmem, hbm, hbm, vmem, vmem, vmem, vmem],
        out_specs=vmem,
        scratch_shapes=[
            pltpu.VMEM((groups, 2, tokens, size), bf16),
            pltpu.VMEM((groups, back, 2, tokens, size), bf16),
            pltpu.VMEM((1, width), f32),
            pltpu.VMEM((slots, 128), f32),
            pltpu.VMEM((back, 1, tokens), jnp.int32),
            pltpu.VMEM((n, groups, tokens, features // groups), bf16),
            pltpu.VMEM((features, columns), bf16),
            pltpu.VMEM((n, half, columns), bf16),
            pltpu.VMEM((n, pieces, 2, half, part), f32),
            pltpu.VMEM((n, pieces, half, part), bf16),
            pltpu.VMEM((n, pieces, half, part), bf16),
            pltpu.VMEM((n, pieces, half, part), bf16),
            pltpu.VMEM((n, pieces, half, part), bf16),
            pltpu.VMEM((exp_count - 1, n, pieces, slots, part), bf16),
            pltpu.VMEM((exp_count, n, pieces, slots, part), bf16),
            dma((1 + n,)),
            dma((groups, back)),
            dma((groups, back)),
            dma((back,)),
            dma((back,)),
            dma((n, groups)),
            dma((n, groups)),
            dma((n, groups)),
            dma((n, pieces)),
            dma((n, pieces)),
            dma((n, pieces)),
            dma((n, pieces)),
            dma((exp_count - 1, n, pieces)),
            dma((exp_count, n, pieces)),
        ],
        compiler_params=pltpu.CompilerParams(collective_id=0, has_side_effects=True),
    )(
        queries[0].transpose(1, 0, 2),
        key_states[0],
        values[0],
        doc_ids,
        stream,
        out_proj,
        norm_gain.reshape(width // 128, 128),
        router.T,
        expert_ids.reshape(1, half),
        keep_counts.reshape(1, experts),
    )
    return out


def solution(mesh):
    placed = (
        P(("groups", "exp"), "ctx", "tp", None),
        P(("groups", "exp"), "ctx", "tp", None),
        P(("groups", "exp"), "ctx", "tp", None),
        P(("groups", "exp"), "ctx"),
        P(("groups", "exp"), ("ctx", "tp"), None),
        P("tp", "ctx"),
        P(),
        P(None, "exp"),
        P(("groups", "exp"), ("ctx", "tp"), None),
        P("groups"),
    )
    return jax.shard_map(
        on_device,
        mesh=mesh,
        in_specs=placed,
        out_specs=P(("groups", "ctx", "tp"), "exp", None, None),
        check_vma=False,
    )
```

```python
import functools
import math

import jax
import jax.numpy as jnp
from jax import lax
from jax.experimental import pallas as pl
from jax.experimental.pallas import tpu as pltpu
from jax.sharding import PartitionSpec as P

CAP = 2
EPSILON = 1e-05
MESH = pl.DeviceIdType.MESH


def kernel(
    sizes,
    q_ref,
    key_ref,
    value_ref,
    doc_ref,
    residual_hbm,
    weight_hbm,
    gain_ref,
    router_ref,
    ids_ref,
    keep_ref,
    out_ref,
    kv_out,
    kv_in,
    gain,
    tally,
    doc_in,
    attn,
    weight,
    residual,
    product,
    part_out,
    part_in,
    res_out,
    res_in,
    slot_out,
    slot_in,
    load_sem,
    kv_send,
    kv_recv,
    doc_send,
    doc_recv,
    right_send,
    left_send,
    attn_recv,
    part_send,
    part_recv,
    res_send,
    res_recv,
    slot_send,
    slot_recv,
):
    ctx_count, exp_count, back, pieces = sizes
    heads, tokens, size = q_ref.shape
    groups = kv_out.shape[0]
    ratio = heads // groups
    half = tokens // 2
    columns = weight.shape[1]
    depth = weight.shape[0] // groups
    slots = slot_in.shape[3]
    part = columns // pieces
    me = lax.axis_index("ctx")
    mine = lax.axis_index("exp")
    core = lax.axis_index("tp")

    load_weight = pltpu.make_async_copy(weight_hbm, weight, load_sem.at[0])
    load_weight.start()
    aligned = columns % 128 == 0
    load_residual = []
    for block in range(ctx_count):
        there = slice(block * columns, (block + 1) * columns)
        load_residual.append(
            pltpu.make_async_copy(
                residual_hbm.at[:, there] if aligned else residual_hbm.at[block],
                residual.at[block],
                load_sem.at[1 + block],
            )
        )
        load_residual[-1].start()

    barrier = pltpu.get_barrier_semaphore()
    for shift in range(1, ctx_count):
        pl.semaphore_signal(
            barrier,
            inc=1,
            device_id={"ctx": lax.rem(me + shift, ctx_count)},
            device_id_type=MESH,
        )
    for shift in range(1, exp_count):
        pl.semaphore_signal(
            barrier,
            inc=1,
            device_id={"exp": lax.rem(mine + shift, exp_count)},
            device_id_type=MESH,
        )
    pl.semaphore_signal(barrier, inc=1, device_id={"tp": 1 - core}, device_id_type=MESH)

    for group in range(groups):
        kv_out[group, 0] = key_ref[:, group, :]
        kv_out[group, 1] = value_ref[:, group, :]

    pl.semaphore_wait(barrier, ctx_count + exp_count - 1)

    def kv_copy(group, shift):
        return pltpu.make_async_remote_copy(
            src_ref=kv_out.at[group],
            dst_ref=kv_in.at[group, shift - 1],
            send_sem=kv_send.at[group, shift - 1],
            recv_sem=kv_recv.at[group, shift - 1],
            device_id={"ctx": lax.rem(me + shift, ctx_count)},
            device_id_type=MESH,
        )

    def doc_copy(shift):
        return pltpu.make_async_remote_copy(
            src_ref=doc_ref,
            dst_ref=doc_in.at[shift - 1],
            send_sem=doc_send.at[shift - 1],
            recv_sem=doc_recv.at[shift - 1],
            device_id={"ctx": lax.rem(me + shift, ctx_count)},
            device_id_type=MESH,
        )

    for shift in range(1, back + 1):

        @pl.when(me + shift < ctx_count)
        def _(shift=shift):
            doc_copy(shift).start()

    for group in range(groups):
        for shift in range(1, back + 1):

            @pl.when(me + shift < ctx_count)
            def _(group=group, shift=shift):
                kv_copy(group, shift).start()

    row = lax.broadcasted_iota(jnp.int32, (half, half), 0)
    lane = lax.broadcasted_iota(jnp.int32, (half, half), 1)
    ids_row = ids_ref[...]
    ids_column = jnp.sum(jnp.where(row == lane, ids_row, 0), axis=1, keepdims=True)
    ranking = jnp.sum(
        jnp.where((ids_column == ids_row) & (row < lane), 1, 0), axis=0, keepdims=True
    )
    experts = keep_ref.shape[1]
    square_row = lax.broadcasted_iota(jnp.int32, (experts, experts), 0)
    square_lane = lax.broadcasted_iota(jnp.int32, (experts, experts), 1)
    keep_column = jnp.sum(
        jnp.where(square_row == square_lane, keep_ref[...], 0), axis=1, keepdims=True
    )
    expert_row = lax.broadcasted_iota(jnp.int32, (experts, half), 0)
    limits = jnp.sum(jnp.where(expert_row == ids_row, keep_column, 0), axis=0, keepdims=True)
    target = jnp.where(ranking < limits, ids_row * CAP + ranking, -1)
    slot_row = lax.broadcasted_iota(jnp.int32, (slots, half), 0)

    wide = gain_ref[...].astype(jnp.float32)
    for line in range(wide.shape[0]):
        gain[:, line * 128 : (line + 1) * 128] = wide[line : line + 1]

    for shift in range(1, back + 1):

        @pl.when(me < shift)
        def _(shift=shift):
            doc_in[shift - 1] = jnp.full(doc_in.shape[1:], -1, jnp.int32)
            for group in range(groups):
                kv_in[group, shift - 1] = jnp.zeros(kv_in.shape[2:], kv_in.dtype)

        @pl.when(me >= shift)
        def _(shift=shift):
            doc_copy(shift).wait_recv()

    square = lax.broadcasted_iota(jnp.int32, (tokens, tokens), 0)
    across = lax.broadcasted_iota(jnp.int32, (tokens, tokens), 1)
    doc_row = doc_ref[...]
    doc_column = jnp.sum(jnp.where(square == across, doc_row, 0), axis=1, keepdims=True)
    allowed = [(across <= square) & (doc_row == doc_column)]
    for shift in range(1, back + 1):
        allowed.append(doc_in[shift - 1] == doc_column)
    allowed = jnp.concatenate(
        [jnp.where(piece, 1.0, 0.0) for piece in allowed], axis=1
    )
    allowed = allowed > 0.5
    scale = 1.0 / math.sqrt(size)

    def attn_copy(block, group, rightward):
        to = me + 1 if rightward else me - 1
        sends = right_send if rightward else left_send
        return pltpu.make_async_remote_copy(
            src_ref=attn.at[block, group],
            dst_ref=attn.at[block, group],
            send_sem=sends.at[block, group],
            recv_sem=attn_recv.at[block, group],
            device_id={"ctx": lax.rem(to + ctx_count, ctx_count)},
            device_id_type=MESH,
        )

    for group in range(groups):
        for shift in range(1, back + 1):

            @pl.when(me >= shift)
            def _(group=group, shift=shift):
                kv_copy(group, shift).wait_recv()

        keys = jnp.concatenate(
            [kv_out[group, 0]] + [kv_in[group, shift, 0] for shift in range(back)], axis=0
        )
        vals = jnp.concatenate(
            [kv_out[group, 1]] + [kv_in[group, shift, 1] for shift in range(back)], axis=0
        )
        for head in range(ratio):
            scores = (
                lax.dot_general(
                    q_ref[group * ratio + head],
                    keys,
                    (((1,), (1,)), ((), ())),
                    preferred_element_type=jnp.float32,
                )
                * scale
            )
            masked = jnp.where(allowed, scores, -1e30)
            highest = jnp.max(masked, axis=1, keepdims=True)
            weights = jnp.where(allowed, jnp.exp(masked - highest), 0.0)
            totals = jnp.sum(weights, axis=1, keepdims=True)
            mixed = jnp.dot(weights.astype(jnp.bfloat16), vals, preferred_element_type=jnp.float32)
            attn[me, group, :, head * size : (head + 1) * size] = (mixed / totals).astype(
                jnp.bfloat16
            )

        @pl.when(me < ctx_count - 1)
        def _(group=group):
            attn_copy(me, group, True).start()

        @pl.when(me > 0)
        def _(group=group):
            attn_copy(me, group, False).start()

    def part_copy(block, piece):
        return pltpu.make_async_remote_copy(
            src_ref=part_out.at[block, piece],
            dst_ref=part_in.at[block, piece],
            send_sem=part_send.at[block, piece],
            recv_sem=part_recv.at[block, piece],
            device_id={"tp": 1 - core},
            device_id_type=MESH,
        )

    def res_copy(block, peer, piece):
        return pltpu.make_async_remote_copy(
            src_ref=res_out.at[block, piece],
            dst_ref=res_in.at[me, piece],
            send_sem=res_send.at[block, piece],
            recv_sem=res_recv.at[peer, piece],
            device_id={"ctx": block},
            device_id_type=MESH,
        )

    def slot_copy(shift, block, peer, piece):
        return pltpu.make_async_remote_copy(
            src_ref=slot_out.at[shift - 1, block, piece],
            dst_ref=slot_in.at[mine, block, piece],
            send_sem=slot_send.at[shift - 1, block, piece],
            recv_sem=slot_recv.at[peer, block, piece],
            device_id={"exp": lax.rem(mine + shift, exp_count)},
            device_id_type=MESH,
        )

    tile = math.gcd(part, 640)

    def project(block, piece):
        for first in range(0, part, tile):
            there = slice(piece * part + first, piece * part + first + tile)
            total = None
            for group in range(groups):
                term = jnp.dot(
                    attn[block, group],
                    weight[group * depth : (group + 1) * depth, there],
                    preferred_element_type=jnp.float32,
                )
                total = term if total is None else total + term
            product[block, piece, 0, :, first : first + tile] = total[:half]
            product[block, piece, 1, :, first : first + tile] = total[half:]
        part_out[block, piece] = product[block, piece, 1 - core].astype(jnp.bfloat16)
        part_copy(block, piece).start()

    def finish(block, piece):
        part_copy(block, piece).wait_recv()
        return (
            product[block, piece, core] + part_in[block, piece].astype(jnp.float32)
        ).astype(jnp.bfloat16)

    def place(block, piece):
        hidden = (
            residual[block, :, piece * part : (piece + 1) * part].astype(jnp.float32)
            + res_in[block, piece].astype(jnp.float32)
        ).astype(jnp.bfloat16)
        for shift in (*range(1, exp_count), 0):
            peer = lax.rem(mine + shift, exp_count)
            table = (slot_row + peer * slots == target).astype(jnp.bfloat16)
            chosen = jnp.dot(table, hidden, preferred_element_type=jnp.float32).astype(
                jnp.bfloat16
            )
            if shift == 0:
                slot_in[mine, block, piece] = chosen
            else:
                slot_out[shift - 1, block, piece] = chosen
                slot_copy(shift, block, mine, piece).start()

    load_weight.wait()
    for piece in range(pieces):
        project(me, piece)
    for load in load_residual:
        load.wait()
    for piece in range(pieces):
        res_in[me, piece] = finish(me, piece)
        place(me, piece)

    def step(distance, carry):
        left, right = me - distance, me + distance
        inside = distance < ctx_count
        has_left = (left >= 0) & inside
        has_right = (right < ctx_count) & inside

        @pl.when(has_left)
        def _():
            for group in range(groups):
                attn_copy(left, group, True).wait_recv()

                @pl.when(me < ctx_count - 1)
                def _():
                    attn_copy(left, group, True).start()

        @pl.when(has_right)
        def _():
            for group in range(groups):
                attn_copy(right, group, False).wait_recv()

                @pl.when(me > 0)
                def _():
                    attn_copy(right, group, False).start()

        for piece in range(pieces):
            for block, has in ((left, has_left), (right, has_right)):

                @pl.when(has)
                def _(block=block):
                    project(block, piece)

        for piece in range(pieces):
            for block, has in ((left, has_left), (right, has_right)):

                @pl.when(has)
                def _(block=block):
                    res_out[block, piece] = finish(block, piece)
                    res_copy(block, me, piece).start()

        for piece in range(pieces):
            for block, ok in (
                (left + 1, (left + 1 >= 0) & (distance >= 2)),
                (right - 1, (right - 1 < ctx_count) & (distance >= 2)),
            ):

                @pl.when(ok)
                def _(block=block):
                    res_copy(me, block, piece).wait_recv()
                    place(block, piece)

        return carry

    lax.fori_loop(1, ctx_count + 1, step, 0)

    spread = lax.broadcasted_iota(jnp.int32, (slots, router_ref.shape[0]), 0) // CAP
    expert = lax.broadcasted_iota(jnp.int32, (slots, router_ref.shape[0]), 1)
    for shift in range(exp_count):
        peer = lax.rem(mine + shift, exp_count)
        tally[...] = jnp.zeros_like(tally)

        def absorb(block):
            for piece in range(pieces):
                if shift:
                    slot_copy(1, block, peer, piece).wait_recv()
                hidden = slot_in[peer, block, piece].astype(jnp.float32)
                tally[:, :1] += jnp.sum(hidden * hidden, axis=1, keepdims=True)

        absorb(me)

        def gather(distance, carry):
            @pl.when(me >= distance)
            def _():
                absorb(me - distance)

            @pl.when(me + distance < ctx_count)
            def _():
                absorb(me + distance)

            return carry

        lax.fori_loop(1, ctx_count, gather, 0)
        factor = lax.rsqrt(tally[:, :1] / (columns * ctx_count) + EPSILON)
        logits = 0.0
        for block in range(ctx_count):
            for piece in range(pieces):
                first = block * columns + piece * part
                there = slice(first, first + part)
                normed = (
                    slot_in[peer, block, piece].astype(jnp.float32) * factor * gain[:, there]
                ).astype(jnp.bfloat16)
                slot_in[peer, block, piece] = normed
                logits = logits + lax.dot_general(
                    normed,
                    router_ref[:, there],
                    (((1,), (1,)), ((), ())),
                    preferred_element_type=jnp.float32,
                )
        logit = jnp.sum(jnp.where(spread == expert, logits, 0.0), axis=1, keepdims=True)
        gate = jax.nn.sigmoid(logit)
        for block in range(ctx_count):
            for piece in range(pieces):
                first = block * columns + piece * part
                done = slot_in[peer, block, piece].astype(jnp.float32) * gate
                out_ref[peer, :, :, first : first + part] = done.reshape(
                    slots // CAP, CAP, part
                ).astype(jnp.bfloat16)

    for shift in range(1, back + 1):

        @pl.when(me + shift < ctx_count)
        def _(shift=shift):
            doc_copy(shift).wait_send()
            for group in range(groups):
                kv_copy(group, shift).wait_send()

    def drain(block, carry):
        for piece in range(pieces):
            part_copy(block, piece).wait_send()
            for shift in range(1, exp_count):
                slot_copy(shift, block, mine, piece).wait_send()

        @pl.when(block != me)
        def _():
            for piece in range(pieces):
                res_copy(block, me, piece).wait_send()

        for group in range(groups):

            @pl.when((block <= me) & (me < ctx_count - 1))
            def _(group=group):
                attn_copy(block, group, True).wait_send()

            @pl.when((block >= me) & (me > 0))
            def _(group=group):
                attn_copy(block, group, False).wait_send()

        return carry

    lax.fori_loop(0, ctx_count, drain, 0)


def on_device(
    queries,
    key_states,
    values,
    doc_ids,
    residual,
    out_proj,
    norm_gain,
    router,
    expert_ids,
    keep_counts,
):
    tokens, heads, size = queries.shape[1:]
    groups = key_states.shape[2]
    ctx_count = lax.axis_size("ctx")
    exp_count = lax.axis_size("exp")
    features, columns = out_proj.shape
    half = residual.shape[1]
    width = residual.shape[2]
    experts = keep_counts.shape[0]
    slots = experts // exp_count * CAP
    longest = tokens * ctx_count // 2
    back = min(ctx_count - 1, -(-(longest - 1) // tokens))
    pieces = 2
    part = columns // pieces
    vmem = pl.BlockSpec(memory_space=pltpu.VMEM)
    hbm = pl.BlockSpec(memory_space=pl.ANY)
    bf16, f32 = jnp.bfloat16, jnp.float32
    dma = pltpu.SemaphoreType.DMA
    n = ctx_count
    stream = residual[0]
    if columns % 128:
        stream = stream.reshape(half, ctx_count, columns).transpose(1, 0, 2)
    out = pl.pallas_call(
        functools.partial(kernel, (ctx_count, exp_count, back, pieces)),
        out_shape=jax.ShapeDtypeStruct((exp_count, slots // CAP, CAP, width), bf16),
        in_specs=[vmem, vmem, vmem, vmem, hbm, hbm, vmem, vmem, vmem, vmem],
        out_specs=vmem,
        scratch_shapes=[
            pltpu.VMEM((groups, 2, tokens, size), bf16),
            pltpu.VMEM((groups, back, 2, tokens, size), bf16),
            pltpu.VMEM((1, width), f32),
            pltpu.VMEM((slots, 128), f32),
            pltpu.VMEM((back, 1, tokens), jnp.int32),
            pltpu.VMEM((n, groups, tokens, features // groups), bf16),
            pltpu.VMEM((features, columns), bf16),
            pltpu.VMEM((n, half, columns), bf16),
            pltpu.VMEM((n, pieces, 2, half, part), f32),
            pltpu.VMEM((n, pieces, half, part), bf16),
            pltpu.VMEM((n, pieces, half, part), bf16),
            pltpu.VMEM((n, pieces, half, part), bf16),
            pltpu.VMEM((n, pieces, half, part), bf16),
            pltpu.VMEM((exp_count - 1, n, pieces, slots, part), bf16),
            pltpu.VMEM((exp_count, n, pieces, slots, part), bf16),
            dma((1 + n,)),
            dma((groups, back)),
            dma((groups, back)),
            dma((back,)),
            dma((back,)),
            dma((n, groups)),
            dma((n, groups)),
            dma((n, groups)),
            dma((n, pieces)),
            dma((n, pieces)),
            dma((n, pieces)),
            dma((n, pieces)),
            dma((exp_count - 1, n, pieces)),
            dma((exp_count, n, pieces)),
        ],
        compiler_params=pltpu.CompilerParams(collective_id=0, has_side_effects=True),
    )(
        queries[0].transpose(1, 0, 2),
        key_states[0],
        values[0],
        doc_ids,
        stream,
        out_proj,
        norm_gain.reshape(width // 128, 128),
        router.T,
        expert_ids.reshape(1, half),
        keep_counts.reshape(1, experts),
    )
    return out


def solution(mesh):
    placed = (
        P(("groups", "exp"), "ctx", "tp", None),
        P(("groups", "exp"), "ctx", "tp", None),
        P(("groups", "exp"), "ctx", "tp", None),
        P(("groups", "exp"), "ctx"),
        P(("groups", "exp"), ("ctx", "tp"), None),
        P("tp", "ctx"),
        P(),
        P(None, "exp"),
        P(("groups", "exp"), ("ctx", "tp"), None),
        P("groups"),
    )
    return jax.shard_map(
        on_device,
        mesh=mesh,
        in_specs=placed,
        out_specs=P(("groups", "ctx", "tp"), "exp", None, None),
        check_vma=False,
    )
```
